128 devices in a mesh: table: 16 (over y, z), seq: 8 (over x, core).
Axes of the slice: x: 4, y: 4, z: 4, core: 2. Of those that a mesh axis runs over, the one named last changes fastest.
Arguments:
- embed_table: bfloat16 [131072, 512], P('table')
- lookup_ids: int32 [16, 8, 16, 192], P('table', 'seq'), may hold values from 0 to 8191
- counts: int32 [16, 8, 16], P('table', 'seq'), may hold values from 0 to 192, as said below
- event_order: int32 [16, 8, 2048], P('table', 'seq'), may hold values from 0 to 2047, each once within a row
- hist_len: int32 [16], P('table'), may hold values from 4096 to 16384, as said below
- w_uvqk: bfloat16 [512, 2048], replicated, may hold values from -0.25 to 0.25
- w_out: bfloat16 [512, 512], replicated, may hold values from -0.25 to 0.25
Outputs:
- layer_out: bfloat16 [16, 16384, 512], P('table', 'seq')
The draws below stay inside these ranges and needn't reach their ends.
Inputs may be any that keep to these rules, and one draw needn't show every extreme that they name: For every user and piece the 16 counts sum to 2048; for every piece index one shard gets exactly 192 from every user. Only the first counts[u, p, j] slots of lookup_ids[u, p, j] are read. `hist_len`: some user has exactly 16384 events.
All inputs are finite; a program needn't handle non-finite values.
Results may differ from the reference program's by a relative error of at most 0.0039.
Values may be sent and summed in bfloat16 or wider, within the bound.
No kernel may reach another device: no remote copies, remote signals or barrier semaphores. Data moves between devices by JAX's collectives and lax.ppermute only.
A program may use at most 128 MiB of HBM per device.

```python
import math
import jax
import jax.numpy as jnp
from jax import lax

D = 512
HEADS = 4
WINDOW = 1024
TOK_DEV = 2048
ROWS_SHARD = 8192
HEAD_DIM = 128
USERS = 16
PIECES = 8
SHARDS = 16
LENGTH = 16384
CAP = 192
ROWS = 131072


def draw_counts(key, part):
    remaining = TOK_DEV - CAP
    base_count = remaining // (SHARDS - 1)
    extra_count = remaining - base_count * (SHARDS - 1)
    key_hot, key_jitter = jax.random.split(jax.random.fold_in(key, 11))
    jitter = jax.random.randint(key_jitter, (USERS, PIECES, SHARDS - 1), 0, base_count // 2 + 1)
    others = base_count + jitter - jnp.roll(jitter, 1, axis=2)
    others = others + (jnp.arange(SHARDS - 1) < extra_count).astype(jnp.int32)[None, None, :]
    hot_shard = jax.random.randint(key_hot, (PIECES,), 0, SHARDS)
    column = jnp.arange(SHARDS)
    source_column = column[None, :] - (column[None, :] > hot_shard[:, None]).astype(jnp.int32)
    source_column = jnp.clip(source_column, 0, SHARDS - 2)
    source_column = jnp.broadcast_to(source_column[None], (USERS, PIECES, SHARDS))
    placed = jnp.take_along_axis(others, source_column, axis=2)
    return jnp.where(column[None, None, :] == hot_shard[None, :, None], CAP, placed).astype(jnp.int32)


def draw_hist_len(key, part):
    key_lengths, key_longest = jax.random.split(jax.random.fold_in(key, 23))
    lengths = jax.random.randint(key_lengths, (USERS,), LENGTH // 4, LENGTH + 1)
    longest = jax.random.randint(key_longest, (), 0, USERS)
    return jnp.where(jnp.arange(USERS) == longest, LENGTH, lengths).astype(jnp.int32)


def draw_embed_table(key, part):
    key_base, key_rows, key_columns = jax.random.split(jax.random.fold_in(key, 37), 3)
    row_scale = jnp.exp(jax.random.uniform(key_rows, (ROWS, 1), minval=math.log(0.3), maxval=math.log(3.0)))
    column_scale = jnp.exp(jax.random.uniform(key_columns, (1, D), minval=math.log(0.3), maxval=math.log(3.0)))
    base_values = jax.random.normal(key_base, (ROWS, D))
    return (base_values * row_scale * column_scale).astype(jnp.float32).astype(jnp.bfloat16)


def plant(entries, stream_key, smallest, high):
    dims = entries.shape
    spot = [jax.random.randint(jax.random.fold_in(stream_key, axis), (), 0, dims[axis]) for axis in range(len(dims))]
    entries = entries.at[tuple(spot)].set(smallest)
    longest = dims.index(max(dims))
    spot[longest] = (spot[longest] + 1) % dims[longest]
    return entries.at[tuple(spot)].set(high)


def normal_values(stream_key, dims, width, most, kind=jnp.bfloat16):
    entries = width * jax.random.normal(stream_key, dims, jnp.float32)
    return jnp.clip(entries, min=-most, max=most).astype(kind)


def setup_inputs(seed: int = 0) -> dict:
    streams_of = jax.random.split(jax.random.key(seed), 8)
    return {
        "embed_table": draw_embed_table(jax.random.fold_in(streams_of[7], 71), 0),
        "lookup_ids": plant(jax.random.randint(streams_of[1], (USERS, PIECES, SHARDS, CAP), 0, ROWS_SHARD), jax.random.fold_in(streams_of[1], 1), 0, ROWS_SHARD - 1).astype(jnp.int32),
        "counts": draw_counts(jax.random.fold_in(streams_of[7], 71), 0),
        "event_order": jax.vmap(lambda own: jax.random.permutation(own, TOK_DEV))(jax.random.split(streams_of[3], USERS * PIECES)).reshape((USERS, PIECES, TOK_DEV)).astype(jnp.int32),
        "hist_len": draw_hist_len(jax.random.fold_in(streams_of[7], 71), 0),
        "w_uvqk": normal_values(streams_of[5], (D, 4 * D), D ** -0.5, 0.25),
        "w_out": normal_values(streams_of[6], (D, D), D ** -0.5, 0.25),
    }


def normalize(values):
    average = lax.optimization_barrier(jnp.mean(values, axis=-1, keepdims=True))
    centered = values - average
    spread = lax.optimization_barrier(jnp.mean(centered * centered, axis=-1, keepdims=True))
    return centered * lax.rsqrt(spread + 1e-05)

def attend_block(queries, keyvals):
    query_rows = queries.shape[0]
    key_rows = keyvals.shape[0]
    query_heads = queries.reshape(query_rows, HEADS, HEAD_DIM).astype(jnp.float32)
    key_heads = keyvals[:, :D].reshape(key_rows, HEADS, HEAD_DIM).astype(jnp.float32)
    value_heads = keyvals[:, D:].reshape(key_rows, HEADS, HEAD_DIM).astype(jnp.float32)
    scores = jnp.einsum('qhd,khd->hqk', query_heads, key_heads) * HEAD_DIM ** (-0.5)
    distance = jnp.arange(query_rows)[:, None] + (key_rows - query_rows) - jnp.arange(key_rows)[None, :]
    inside = (distance >= 0) & (distance < key_rows - query_rows)
    weights = jnp.where(inside[None], jax.nn.silu(scores), 0.0).astype(jnp.bfloat16)
    attended = jnp.einsum('hqk,khd->qhd', weights.astype(jnp.float32), value_heads)
    return attended.reshape(query_rows, D)

def gather_events(embed_table, lookup_ids, counts, event_order):
    totals = jnp.cumsum(counts, axis=2)
    starts = totals - counts
    owner_shard = lax.optimization_barrier(jnp.sum((event_order[..., None] >= totals[:, :, None, :]).astype(jnp.int32), axis=3))
    slot_start = jnp.take_along_axis(starts, owner_shard, axis=2)
    slot_index = (owner_shard * CAP + event_order - slot_start).astype(jnp.int32)
    flat_ids = lookup_ids.reshape(USERS, PIECES, SHARDS * CAP)
    local_ids = jnp.take_along_axis(flat_ids, slot_index, axis=2)
    table_rows = (owner_shard * ROWS_SHARD + local_ids).astype(jnp.int32)
    return embed_table[table_rows.reshape(USERS, LENGTH)]

def user_layer(embedded, length, w_uvqk, w_out):
    normed = normalize(embedded.astype(jnp.float32)).astype(jnp.bfloat16)
    activated = jax.nn.silu(jnp.dot(normed, w_uvqk, preferred_element_type=jnp.float32)).astype(jnp.bfloat16)
    gate_part = activated[:, :D]
    queries = activated[:, D:2 * D]
    keyvals = activated[:, 2 * D:]
    padded = jnp.concatenate([jnp.zeros((WINDOW, 2 * D), jnp.bfloat16), keyvals], axis=0)

    def one_block(block_index):
        first = (block_index * WINDOW).astype(jnp.int32)
        query_block = lax.dynamic_slice_in_dim(queries, first, WINDOW, 0)
        key_block = lax.dynamic_slice_in_dim(padded, first, 2 * WINDOW, 0)
        return attend_block(query_block, key_block)
    attended = lax.map(one_block, jnp.arange(LENGTH // WINDOW, dtype=jnp.int32)).reshape(LENGTH, D)
    gated_rows = (normalize(attended) * gate_part.astype(jnp.float32)).astype(jnp.bfloat16)
    result = jnp.dot(gated_rows, w_out, preferred_element_type=jnp.float32) + embedded.astype(jnp.float32)
    inside = jnp.arange(LENGTH, dtype=jnp.int32) < length
    return jnp.where(inside[:, None], result, 0.0).astype(jnp.bfloat16)

def reference(embed_table, lookup_ids, counts, event_order, hist_len, w_uvqk, w_out):
    events = gather_events(embed_table, lookup_ids, counts, event_order)

    def per_user(user_pair):
        return user_layer(user_pair[0], user_pair[1], w_uvqk, w_out)
    return lax.map(per_user, (events, hist_len))
```

```python
import jax
import jax.numpy as jnp
from jax import lax
from jax.experimental import pallas as pl
from jax.experimental.pallas import tpu as pltpu
from jax.sharding import PartitionSpec as P

HEADS = 4
WINDOW = 1024
TILE = 256
LANES = 128
MIB = 1 << 20
F32 = jnp.float32
BF16 = jnp.bfloat16
VMEM = pl.BlockSpec(memory_space=pltpu.VMEM)
SMEM = pl.BlockSpec(memory_space=pltpu.SMEM)
ANY = pl.BlockSpec(memory_space=pl.ANY)


def passed_along(value, axis, steps):
    count = lax.axis_size(axis)
    initial, last = (max(0, -steps), min(count, count - steps))
    return lax.ppermute(value, axis, [(source, source + steps) for source in range(initial, last)])


def normalize(values):
    average = jnp.mean(values, axis=-1, keepdims=True)
    centered = values - average
    spread = jnp.mean(centered * centered, axis=-1, keepdims=True)
    return centered * lax.rsqrt(spread + 1e-05)


def silu(values, scale=1.0):
    half = values * (0.5 * scale)
    return half + half * jnp.tanh(half)


def dot(a, b):
    return jnp.dot(a, b, preferred_element_type=F32)


def dot_nt(a, b):
    return lax.dot_general(a, b, (((1,), (1,)), ((), ())), preferred_element_type=F32)


def spread_rows(source, target, first, count):
    step = 32
    parts = source.shape[1] // LANES

    @pl.loop(0, count // step)
    def _(i):
        row = pl.multiple_of(first + i * step, step)
        block = source[pl.ds(row, step), :].astype(F32)
        for k in range(parts):
            target[pl.ds(parts * row + k, step, stride=parts), :] = block[
                :, k * LANES : (k + 1) * LANES
            ]


def pick_rows(indices, source, target, count, parts):
    unroll = 32

    @pl.loop(0, count // unroll)
    def _(i):
        for u in range(unroll):
            j = i * unroll + u
            r = indices[j]
            target[pl.ds(pl.multiple_of(parts * j, parts), parts), :] = source[
                pl.ds(pl.multiple_of(parts * r, parts), parts), :
            ]


def join_rows(source, target, first, count, parts):
    step = 32

    @pl.loop(0, count // step)
    def _(i):
        row = pl.multiple_of(i * step, step)
        for k in range(parts):
            target[pl.ds(row, step), k * LANES : (k + 1) * LANES] = source[
                pl.ds(parts * (first + row) + k, step, stride=parts), :
            ].astype(BF16)


def gather_rows(table, ids):
    rows, width = table.shape
    count = ids.shape[0]
    parts = width // LANES
    chunks = 8
    size = rows // chunks

    def kernel(ids_ref, table_ref, out_ref, held, wide, picked, sems):
        copies = [
            pltpu.make_async_copy(
                table_ref.at[pl.ds(c * size, size)], held.at[pl.ds(c * size, size)], sems.at[c]
            )
            for c in range(chunks)
        ]
        for copy in copies:
            copy.start()
        for c in range(chunks):
            copies[c].wait()
            spread_rows(held, wide, c * size, size)
        pick_rows(ids_ref, wide, picked, count, parts)
        join_rows(picked, out_ref, 0, count, parts)

    return pl.pallas_call(
        kernel,
        out_shape=jax.ShapeDtypeStruct((count, width), BF16),
        in_specs=[SMEM, ANY],
        out_specs=VMEM,
        scratch_shapes=[
            pltpu.VMEM((rows, width), BF16),
            pltpu.VMEM((rows * parts, LANES), F32),
            pltpu.VMEM((count * parts, LANES), F32),
            pltpu.SemaphoreType.DMA((chunks,)),
        ],
        compiler_params=pltpu.CompilerParams(vmem_limit_bytes=40 * MIB),
        name="gather_rows",
    )(ids, table)


def order_rows(fetched, slots):
    count, width = fetched.shape
    tokens = slots.shape[0]
    parts = width // LANES
    chunks = 6
    size = count // chunks
    half = tokens // 2

    def kernel(slots_ref, rows_ref, low_ref, high_ref, held, wide, picked, sems):
        copies = [
            pltpu.make_async_copy(
                rows_ref.at[pl.ds(c * size, size)], held.at[pl.ds(c * size, size)], sems.at[c]
            )
            for c in range(chunks)
        ]
        for copy in copies:
            copy.start()
        for c in range(chunks):
            copies[c].wait()
            spread_rows(held, wide, c * size, size)
        pick_rows(slots_ref, wide, picked, tokens, parts)
        join_rows(picked, low_ref, 0, half, parts)
        join_rows(picked, high_ref, half, half, parts)

    out = jax.ShapeDtypeStruct((half, width), BF16)
    return pl.pallas_call(
        kernel,
        out_shape=(out, out),
        in_specs=[SMEM, ANY],
        out_specs=(VMEM, VMEM),
        scratch_shapes=[
            pltpu.VMEM((count, width), BF16),
            pltpu.VMEM((count * parts, LANES), F32),
            pltpu.VMEM((tokens * parts, LANES), F32),
            pltpu.SemaphoreType.DMA((chunks,)),
        ],
        compiler_params=pltpu.CompilerParams(vmem_limit_bytes=32 * MIB),
        name="order_rows",
    )(slots, fetched)


def lower_mask():
    row = lax.broadcasted_iota(jnp.int32, (TILE, TILE), 0)
    column = lax.broadcasted_iota(jnp.int32, (TILE, TILE), 1)
    return column <= row


def finish(attended, gate, events, w_out, limit, first):
    gated = (normalize(attended) * gate.astype(F32)).astype(BF16)
    result = dot(gated, w_out) + events.astype(F32)
    position = first + lax.broadcasted_iota(jnp.int32, result.shape, 0)
    return jnp.where(position < limit, result, 0.0).astype(BF16)


def own_part(limit, low, high, w_uvqk, w_out):
    half, width = low.shape
    tokens = 2 * half
    head = width // HEADS
    scale = head ** (-0.5)
    reach = WINDOW // TILE
    tiles = tokens // TILE

    def kernel(
        limit_ref, low_ref, high_ref, w_ref, wo_ref, out_ref, part_ref, query_ref, gate_ref, act, done, sem
    ):
        for source, first in ((low_ref, 0), (high_ref, half)):

            @pl.loop(0, half // TILE)
            def _(i):
                row = pl.multiple_of(i * TILE, TILE)
                normed = normalize(source[pl.ds(row, TILE), :].astype(F32)).astype(BF16)
                for k in range(4):
                    cols = slice(k * width, (k + 1) * width)
                    act[pl.ds(first + row, TILE), cols] = silu(dot(normed, w_ref[:, cols])).astype(BF16)

        mask = lower_mask()

        def cols_of(k, h):
            return slice(k * width + h * head, k * width + (h + 1) * head)

        for t in range(reach):
            rows = slice(t * TILE, (t + 1) * TILE)
            for h in range(HEADS):
                query = act[rows, cols_of(1, h)]
                scores = dot_nt(query, act[0 : (t + 1) * TILE, cols_of(2, h)])
                weights = silu(scores, scale)
                diagonal = jnp.where(mask, weights[:, t * TILE :], 0.0).astype(BF16)
                total = dot(diagonal, act[rows, cols_of(3, h)])
                if t:
                    total += dot(weights[:, : t * TILE].astype(BF16), act[0 : t * TILE, cols_of(3, h)])
                part_ref[rows, h * head : (h + 1) * head] = total
        query_ref[...] = act[0:half, width : 2 * width]
        gate_ref[...] = act[0:half, 0:width]

        @pl.loop(0, tiles - reach)
        def _(i):
            t = i + reach
            row = pl.multiple_of(t * TILE, TILE)
            back = pl.multiple_of(i * TILE, TILE)
            pieces = []
            for h in range(HEADS):
                query = act[pl.ds(row, TILE), cols_of(1, h)]
                edge = dot_nt(query, act[pl.ds(back, TILE), cols_of(2, h)])
                inner = dot_nt(query, act[pl.ds(back + TILE, WINDOW - TILE), cols_of(2, h)])
                last = dot_nt(query, act[pl.ds(row, TILE), cols_of(2, h)])
                both = silu(jnp.where(mask, last, edge), scale)
                total = dot(
                    silu(inner, scale).astype(BF16),
                    act[pl.ds(back + TILE, WINDOW - TILE), cols_of(3, h)],
                )
                total += dot(
                    jnp.where(mask, both, 0.0).astype(BF16), act[pl.ds(row, TILE), cols_of(3, h)]
                )
                total += dot(
                    jnp.where(mask, 0.0, both).astype(BF16), act[pl.ds(back, TILE), cols_of(3, h)]
                )
                pieces.append(total)
            done[pl.ds(back, TILE), :] = finish(
                jnp.concatenate(pieces, axis=1),
                act[pl.ds(row, TILE), 0:width],
                high_ref[pl.ds(back, TILE), :],
                wo_ref[...],
                limit_ref[0],
                row,
            )

        copy = pltpu.make_async_copy(done, out_ref.at[pl.ds(half, half)], sem)
        copy.start()
        copy.wait()

    return pl.pallas_call(
        kernel,
        out_shape=(
            jax.ShapeDtypeStruct((tokens, width), BF16),
            jax.ShapeDtypeStruct((half, width), F32),
            jax.ShapeDtypeStruct((half, width), BF16),
            jax.ShapeDtypeStruct((half, width), BF16),
        ),
        in_specs=[SMEM, VMEM, VMEM, VMEM, VMEM],
        out_specs=(ANY, VMEM, VMEM, VMEM),
        scratch_shapes=[
            pltpu.VMEM((tokens, 4 * width), BF16),
            pltpu.VMEM((half, width), BF16),
            pltpu.SemaphoreType.DMA,
        ],
        compiler_params=pltpu.CompilerParams(vmem_limit_bytes=36 * MIB),
        cost_estimate=pl.CostEstimate(
            flops=14_000_000_000, bytes_accessed=12_000_000, transcendentals=12_000_000
        ),
        name="own_part",
    )(limit, low, high, w_uvqk, w_out)


def halo_part(limit, before, part, query, gate, low, w_uvqk, w_out, out):
    half, width = low.shape
    head = width // HEADS
    scale = head ** (-0.5)
    reach = WINDOW // TILE

    def kernel(
        limit_ref, before_ref, part_ref, query_ref, gate_ref, low_ref, w_ref, wo_ref, _, out_ref, keyvals, done, sem
    ):
        @pl.loop(0, half // TILE)
        def _(i):
            row = pl.multiple_of(i * TILE, TILE)
            normed = normalize(before_ref[pl.ds(row, TILE), :].astype(F32)).astype(BF16)
            for k in range(2):
                cols = slice((k + 2) * width, (k + 3) * width)
                keyvals[pl.ds(row, TILE), k * width : (k + 1) * width] = silu(
                    dot(normed, w_ref[:, cols])
                ).astype(BF16)

        mask = lower_mask()
        for t in range(reach):
            rows = slice(t * TILE, (t + 1) * TILE)
            pieces = []
            for h in range(HEADS):
                cols = slice(h * head, (h + 1) * head)
                vcols = slice(width + h * head, width + (h + 1) * head)
                weights = silu(dot_nt(query_ref[rows, cols], keyvals[t * TILE :, cols]), scale)
                edge = jnp.where(mask, 0.0, weights[:, :TILE]).astype(BF16)
                total = part_ref[rows, cols] + dot(edge, keyvals[rows, vcols])
                if t + 1 < reach:
                    total += dot(weights[:, TILE:].astype(BF16), keyvals[(t + 1) * TILE :, vcols])
                pieces.append(total)
            done[rows, :] = finish(
                jnp.concatenate(pieces, axis=1),
                gate_ref[rows, :],
                low_ref[rows, :],
                wo_ref[...],
                limit_ref[0],
                t * TILE,
            )
        copy = pltpu.make_async_copy(done, out_ref.at[pl.ds(0, half)], sem)
        copy.start()
        copy.wait()

    return pl.pallas_call(
        kernel,
        out_shape=jax.ShapeDtypeStruct(out.shape, out.dtype),
        in_specs=[SMEM, VMEM, VMEM, VMEM, VMEM, VMEM, VMEM, VMEM, ANY],
        out_specs=ANY,
        scratch_shapes=[
            pltpu.VMEM((half, 2 * width), BF16),
            pltpu.VMEM((half, width), BF16),
            pltpu.SemaphoreType.DMA,
        ],
        input_output_aliases={8: 0},
        compiler_params=pltpu.CompilerParams(vmem_limit_bytes=36 * MIB),
        name="halo_part",
    )(limit, before, part, query, gate, low, w_uvqk, w_out, out)


def local(embed_table, lookup_ids, counts, event_order, hist_len, w_uvqk, w_out):
    shards = lax.axis_size("table")
    capacity = lookup_ids.shape[3]
    tokens = event_order.shape[2]
    width = embed_table.shape[1]
    requests = lax.all_to_all(lookup_ids[0, 0], "table", split_axis=0, concat_axis=0, tiled=True)
    requests = jnp.clip(requests.reshape(shards * capacity), 0, embed_table.shape[0] - 1)
    found = gather_rows(embed_table, requests)
    fetched = lax.all_to_all(
        found.reshape(shards, capacity, width), "table", split_axis=0, concat_axis=0, tiled=True
    )
    live_counts = counts[0, 0]
    totals = jnp.cumsum(live_counts)
    starts = totals - live_counts
    event_rank = event_order[0, 0]
    owner_shard = jnp.sum((event_rank[:, None] >= totals[None, :]).astype(jnp.int32), axis=1)
    chosen = owner_shard[:, None] == jnp.arange(shards, dtype=jnp.int32)[None, :]
    slot_start = jnp.sum(jnp.where(chosen, starts[None, :], 0), axis=1)
    slot_index = owner_shard * capacity + event_rank - slot_start
    low, high = order_rows(fetched.reshape(shards * capacity, width), slot_index)
    before = passed_along(high, "seq", 1)
    limit = hist_len - lax.axis_index("seq") * tokens
    out, part, query, gate = own_part(limit, low, high, w_uvqk, w_out)
    result = halo_part(limit, before, part, query, gate, low, w_uvqk, w_out, out)
    return result[None]


def solution(mesh):
    in_specs = (
        P("table", None),
        P("table", "seq", None, None),
        P("table", "seq", None),
        P("table", "seq", None),
        P("table"),
        P(),
        P(),
    )
    out_specs = P("table", "seq", None)
    return jax.shard_map(local, mesh=mesh, in_specs=in_specs, out_specs=out_specs, check_vma=False)
```

```python
import jax
import jax.numpy as jnp
from jax import lax
from jax.experimental import pallas as pl
from jax.experimental.pallas import tpu as pltpu
from jax.sharding import PartitionSpec as P

HEADS = 4
WINDOW = 1024
TILE = 256
LANES = 128
MIB = 1 << 20
F32 = jnp.float32
BF16 = jnp.bfloat16
VMEM = pl.BlockSpec(memory_space=pltpu.VMEM)
SMEM = pl.BlockSpec(memory_space=pltpu.SMEM)
ANY = pl.BlockSpec(memory_space=pl.ANY)


def passed_along(value, axis, steps):
    count = lax.axis_size(axis)
    initial, last = (max(0, -steps), min(count, count - steps))
    return lax.ppermute(value, axis, [(source, source + steps) for source in range(initial, last)])


def normalize(values):
    average = jnp.mean(values, axis=-1, keepdims=True)
    centered = values - average
    spread = jnp.mean(centered * centered, axis=-1, keepdims=True)
    return centered * lax.rsqrt(spread + 1e-05)


def silu(values, scale=1.0):
    half = values * (0.5 * scale)
    return half + half * jnp.tanh(half)


def dot(a, b):
    return jnp.dot(a, b, preferred_element_type=F32)


def dot_nt(a, b):
    return lax.dot_general(a, b, (((1,), (1,)), ((), ())), preferred_element_type=F32)


def spread_rows(source, target, first, count, base=0):
    step = 32
    parts = source.shape[1] // LANES

    @pl.loop(0, count // step)
    def _(i):
        row = pl.multiple_of(first + i * step, step)
        block = source[pl.ds(row, step), :].astype(F32)
        for k in range(parts):
            target[pl.ds(parts * (base + row) + k, step, stride=parts), :] = block[
                :, k * LANES : (k + 1) * LANES
            ]


def pick_row(place, source, target, j, parts):
    target[pl.ds(pl.multiple_of(parts * j, parts), parts), :] = source[
        pl.ds(pl.multiple_of(place, parts), parts), :
    ]


def join_rows(source, target, first, count, parts):
    step = 32

    @pl.loop(0, count // step)
    def _(i):
        row = pl.multiple_of(i * step, step)
        for k in range(parts):
            target[pl.ds(row, step), k * LANES : (k + 1) * LANES] = source[
                pl.ds(parts * (first + row) + k, step, stride=parts), :
            ].astype(BF16)


def gather_rows(table, places, users, count, stride):
    rows, width = table.shape
    parts = width // LANES
    chunks = 8
    size = rows // chunks
    unroll = 32 if count % 32 == 0 else 16

    def kernel(places_ref, table_ref, out_ref, near, held, wide, picked, joined, near_sem, in_sems, out_sems):
        loads = [
            pltpu.make_async_copy(
                table_ref.at[pl.ds(c * size, size)], held.at[pl.ds(c * size, size)], in_sems.at[c]
            )
            for c in range(chunks)
        ]
        stores = [
            pltpu.make_async_copy(joined.at[user], out_ref.at[user], out_sems.at[user])
            for user in range(users)
        ]
        indices = pltpu.make_async_copy(places_ref, near, near_sem)
        for load in loads:
            load.start()
        indices.start()
        for c in range(chunks):
            loads[c].wait()
            spread_rows(held, wide, c * size, size)
        indices.wait()
        for user in range(users):

            @pl.loop(0, count // unroll)
            def _(i):
                for u in range(unroll):
                    o = i * unroll + u
                    pick_row(near[user * stride + o], wide, picked, user * count + o, parts)

            join_rows(picked, joined.at[user], user * count, count, parts)
            stores[user].start()
        for store in stores:
            store.wait()

    return pl.pallas_call(
        kernel,
        out_shape=jax.ShapeDtypeStruct((users, count, width), BF16),
        in_specs=[ANY, ANY],
        out_specs=ANY,
        scratch_shapes=[
            pltpu.SMEM((users * stride,), jnp.int32),
            pltpu.VMEM((rows, width), BF16),
            pltpu.VMEM((rows * parts, LANES), F32),
            pltpu.VMEM((users * count * parts, LANES), F32),
            pltpu.VMEM((users, count, width), BF16),
            pltpu.SemaphoreType.DMA,
            pltpu.SemaphoreType.DMA((chunks,)),
            pltpu.SemaphoreType.DMA((users,)),
        ],
        compiler_params=pltpu.CompilerParams(vmem_limit_bytes=62 * MIB),
        name="gather_rows",
    )(places, table)


def order_rows(fetched, places):
    count, width = fetched.shape
    tokens = places.shape[0]
    parts = width // LANES
    half = tokens // 2

    def kernel(places_ref, rows_ref, low_ref, high_ref, wide, picked):
        spread_rows(rows_ref, wide, 0, count)
        unroll = 32

        @pl.loop(0, tokens // unroll)
        def _(i):
            for u in range(unroll):
                j = i * unroll + u
                pick_row(places_ref[j], wide, picked, j, parts)

        join_rows(picked, low_ref, 0, half, parts)
        join_rows(picked, high_ref, half, half, parts)

    out = jax.ShapeDtypeStruct((half, width), BF16)
    return pl.pallas_call(
        kernel,
        out_shape=(out, out),
        in_specs=[SMEM, VMEM],
        out_specs=(VMEM, VMEM),
        scratch_shapes=[
            pltpu.VMEM((count * parts, LANES), F32),
            pltpu.VMEM((tokens * parts, LANES), F32),
        ],
        compiler_params=pltpu.CompilerParams(vmem_limit_bytes=24 * MIB),
        name="order_rows",
    )(places, fetched)


def lower_mask():
    row = lax.broadcasted_iota(jnp.int32, (TILE, TILE), 0)
    column = lax.broadcasted_iota(jnp.int32, (TILE, TILE), 1)
    return column <= row


def finish(attended, gate, events, w_out, limit, first):
    gated = (normalize(attended) * gate.astype(F32)).astype(BF16)
    result = dot(gated, w_out) + events.astype(F32)
    position = first + lax.broadcasted_iota(jnp.int32, result.shape, 0)
    return jnp.where(position < limit, result, 0.0).astype(BF16)


def own_part(limit, low, high, w_uvqk, w_out):
    half, width = low.shape
    tokens = 2 * half
    head = width // HEADS
    scale = head ** (-0.5)
    reach = WINDOW // TILE
    tiles = tokens // TILE

    def kernel(
        limit_ref, low_ref, high_ref, w_ref, wo_ref, out_ref, part_ref, query_ref, gate_ref, act, done, sem
    ):
        for source, first in ((low_ref, 0), (high_ref, half)):

            @pl.loop(0, half // TILE, unroll=True)
            def _(i):
                row = pl.multiple_of(i * TILE, TILE)
                normed = normalize(source[pl.ds(row, TILE), :].astype(F32)).astype(BF16)
                for k in range(4):
                    cols = slice(k * width, (k + 1) * width)
                    act[pl.ds(first + row, TILE), cols] = silu(dot(normed, w_ref[:, cols])).astype(BF16)

        mask = lower_mask()

        def cols_of(k, h):
            return slice(k * width + h * head, k * width + (h + 1) * head)

        for t in range(reach):
            rows = slice(t * TILE, (t + 1) * TILE)
            for h in range(HEADS):
                query = act[rows, cols_of(1, h)]
                scores = dot_nt(query, act[0 : (t + 1) * TILE, cols_of(2, h)])
                weights = silu(scores, scale)
                diagonal = jnp.where(mask, weights[:, t * TILE :], 0.0).astype(BF16)
                total = dot(diagonal, act[rows, cols_of(3, h)])
                if t:
                    total += dot(weights[:, : t * TILE].astype(BF16), act[0 : t * TILE, cols_of(3, h)])
                part_ref[rows, h * head : (h + 1) * head] = total
        query_ref[...] = act[0:half, width : 2 * width]
        gate_ref[...] = act[0:half, 0:width]

        @pl.loop(0, tiles - reach, unroll=True)
        def _(i):
            t = i + reach
            row = pl.multiple_of(t * TILE, TILE)
            back = pl.multiple_of(i * TILE, TILE)
            pieces = []
            for h in range(HEADS):
                query = act[pl.ds(row, TILE), cols_of(1, h)]
                edge = dot_nt(query, act[pl.ds(back, TILE), cols_of(2, h)])
                inner = dot_nt(query, act[pl.ds(back + TILE, WINDOW - TILE), cols_of(2, h)])
                last = dot_nt(query, act[pl.ds(row, TILE), cols_of(2, h)])
                both = silu(jnp.where(mask, last, edge), scale)
                total = dot(
                    silu(inner, scale).astype(BF16),
                    act[pl.ds(back + TILE, WINDOW - TILE), cols_of(3, h)],
                )
                total += dot(
                    jnp.where(mask, both, 0.0).astype(BF16), act[pl.ds(row, TILE), cols_of(3, h)]
                )
                total += dot(
                    jnp.where(mask, 0.0, both).astype(BF16), act[pl.ds(back, TILE), cols_of(3, h)]
                )
                pieces.append(total)
            done[pl.ds(back, TILE), :] = finish(
                jnp.concatenate(pieces, axis=1),
                act[pl.ds(row, TILE), 0:width],
                high_ref[pl.ds(back, TILE), :],
                wo_ref[...],
                limit_ref[0],
                row,
            )

        copy = pltpu.make_async_copy(done, out_ref.at[pl.ds(half, half)], sem)
        copy.start()
        copy.wait()

    return pl.pallas_call(
        kernel,
        out_shape=(
            jax.ShapeDtypeStruct((tokens, width), BF16),
            jax.ShapeDtypeStruct((half, width), F32),
            jax.ShapeDtypeStruct((half, width), BF16),
            jax.ShapeDtypeStruct((half, width), BF16),
        ),
        in_specs=[SMEM, VMEM, VMEM, VMEM, VMEM],
        out_specs=(ANY, VMEM, VMEM, VMEM),
        scratch_shapes=[
            pltpu.VMEM((tokens, 4 * width), BF16),
            pltpu.VMEM((half, width), BF16),
            pltpu.SemaphoreType.DMA,
        ],
        compiler_params=pltpu.CompilerParams(vmem_limit_bytes=36 * MIB),
        cost_estimate=pl.CostEstimate(
            flops=14_000_000_000, bytes_accessed=12_000_000, transcendentals=12_000_000
        ),
        name="own_part",
    )(limit, low, high, w_uvqk, w_out)


def halo_part(limit, before, part, query, gate, low, w_uvqk, w_out, out):
    half, width = low.shape
    head = width // HEADS
    scale = head ** (-0.5)
    reach = WINDOW // TILE

    def kernel(
        limit_ref, before_ref, part_ref, query_ref, gate_ref, low_ref, w_ref, wo_ref, _, out_ref, keyvals, done, sem
    ):
        @pl.loop(0, half // TILE, unroll=True)
        def _(i):
            row = pl.multiple_of(i * TILE, TILE)
            normed = normalize(before_ref[pl.ds(row, TILE), :].astype(F32)).astype(BF16)
            for k in range(2):
                cols = slice((k + 2) * width, (k + 3) * width)
                keyvals[pl.ds(row, TILE), k * width : (k + 1) * width] = silu(
                    dot(normed, w_ref[:, cols])
                ).astype(BF16)

        mask = lower_mask()
        for t in range(reach):
            rows = slice(t * TILE, (t + 1) * TILE)
            pieces = []
            for h in range(HEADS):
                cols = slice(h * head, (h + 1) * head)
                vcols = slice(width + h * head, width + (h + 1) * head)
                weights = silu(dot_nt(query_ref[rows, cols], keyvals[t * TILE :, cols]), scale)
                edge = jnp.where(mask, 0.0, weights[:, :TILE]).astype(BF16)
                total = part_ref[rows, cols] + dot(edge, keyvals[rows, vcols])
                if t + 1 < reach:
                    total += dot(weights[:, TILE:].astype(BF16), keyvals[(t + 1) * TILE :, vcols])
                pieces.append(total)
            done[rows, :] = finish(
                jnp.concatenate(pieces, axis=1),
                gate_ref[rows, :],
                low_ref[rows, :],
                wo_ref[...],
                limit_ref[0],
                t * TILE,
            )
        copy = pltpu.make_async_copy(done, out_ref.at[pl.ds(0, half)], sem)
        copy.start()
        copy.wait()

    return pl.pallas_call(
        kernel,
        out_shape=jax.ShapeDtypeStruct(out.shape, out.dtype),
        in_specs=[SMEM, VMEM, VMEM, VMEM, VMEM, VMEM, VMEM, VMEM, ANY],
        out_specs=ANY,
        scratch_shapes=[
            pltpu.VMEM((half, 2 * width), BF16),
            pltpu.VMEM((half, width), BF16),
            pltpu.SemaphoreType.DMA,
        ],
        input_output_aliases={8: 0},
        compiler_params=pltpu.CompilerParams(vmem_limit_bytes=36 * MIB),
        name="halo_part",
    )(limit, before, part, query, gate, low, w_uvqk, w_out, out)


def local(embed_table, lookup_ids, counts, event_order, hist_len, w_uvqk, w_out):
    shards = lax.axis_size("table")
    capacity = lookup_ids.shape[3]
    tokens = event_order.shape[2]
    width = embed_table.shape[1]
    parts = width // LANES
    exchange = lambda rows: lax.all_to_all(rows, "table", split_axis=0, concat_axis=0, tiled=True)
    stride = -(-capacity // LANES) * LANES
    starts_in_wide = jnp.pad(parts * lookup_ids[0, 0], ((0, 0), (0, stride - capacity)))
    requests = exchange(starts_in_wide.reshape(shards, stride // LANES, LANES)).reshape(shards * stride)
    fetched = exchange(gather_rows(embed_table, requests, shards, capacity, stride))
    live_counts = counts[0, 0]
    totals = jnp.cumsum(live_counts)
    starts = totals - live_counts
    event_rank = event_order[0, 0]
    owner_shard = jnp.sum((event_rank[:, None] >= totals[None, :]).astype(jnp.int32), axis=1)
    chosen = owner_shard[:, None] == jnp.arange(shards, dtype=jnp.int32)[None, :]
    slot_start = jnp.sum(jnp.where(chosen, starts[None, :], 0), axis=1)
    place = owner_shard * capacity + event_rank - slot_start
    low, high = order_rows(fetched.reshape(shards * capacity, width), parts * place)
    before = passed_along(high, "seq", 1)
    limit = hist_len - lax.axis_index("seq") * tokens
    out, part, query, gate = own_part(limit, low, high, w_uvqk, w_out)
    result = halo_part(limit, before, part, query, gate, low, w_uvqk, w_out, out)
    return result[None]


def solution(mesh):
    in_specs = (
        P("table", None),
        P("table", "seq", None, None),
        P("table", "seq", None),
        P("table", "seq", None),
        P("table"),
        P(),
        P(),
    )
    out_specs = P("table", "seq", None)
    return jax.shard_map(local, mesh=mesh, in_specs=in_specs, out_specs=out_specs, check_vma=False)
```

```python
import jax
import jax.numpy as jnp
from jax import lax
from jax.experimental import pallas as pl
from jax.experimental.pallas import tpu as pltpu
from jax.sharding import PartitionSpec as P

HEADS = 4
WINDOW = 1024
TILE = 256
LANES = 128
MIB = 1 << 20
F32 = jnp.float32
BF16 = jnp.bfloat16
VMEM = pl.BlockSpec(memory_space=pltpu.VMEM)
SMEM = pl.BlockSpec(memory_space=pltpu.SMEM)
ANY = pl.BlockSpec(memory_space=pl.ANY)
HBM = pl.BlockSpec(memory_space=pltpu.HBM)


def passed_along(value, axis, steps):
    count = lax.axis_size(axis)
    initial, last = (max(0, -steps), min(count, count - steps))
    return lax.ppermute(value, axis, [(source, source + steps) for source in range(initial, last)])


def normalize(values, factor=1.0):
    average = jnp.mean(values, axis=-1, keepdims=True)
    centered = values - average
    spread = jnp.mean(centered * centered, axis=-1, keepdims=True)
    return centered * (factor * lax.rsqrt(spread + 1e-05))


def silu_of_twice(half):
    return half + half * jnp.tanh(half)


def dot(a, b):
    return jnp.dot(a, b, preferred_element_type=F32)


def dot_nt(a, b):
    return lax.dot_general(a, b, (((1,), (1,)), ((), ())), preferred_element_type=F32)


def spread_rows(source, target, first, count, base=0):
    step = 32
    parts = source.shape[1] // LANES

    @pl.loop(0, count // step)
    def _(i):
        row = pl.multiple_of(first + i * step, step)
        block = source[pl.ds(row, step), :].astype(F32)
        for k in range(parts):
            target[pl.ds(parts * (base + row) + k, step, stride=parts), :] = block[
                :, k * LANES : (k + 1) * LANES
            ]


def pick_row(place, source, target, j, parts):
    target[pl.ds(pl.multiple_of(parts * j, parts), parts), :] = source[
        pl.ds(pl.multiple_of(place, parts), parts), :
    ]


def join_rows(source, target, first, count, parts):
    step = 32

    @pl.loop(0, count // step)
    def _(i):
        row = pl.multiple_of(i * step, step)
        for k in range(parts):
            target[pl.ds(row, step), k * LANES : (k + 1) * LANES] = source[
                pl.ds(parts * (first + row) + k, step, stride=parts), :
            ].astype(BF16)


def gather_rows(table, places, users, count, stride):
    rows, width = table.shape
    parts = width // LANES
    chunks = 8
    size = rows // chunks
    unroll = 32 if count % 32 == 0 else 16

    def kernel(places_ref, table_ref, out_ref, near, held, wide, picked, joined, near_sem, in_sems, out_sems):
        loads = [
            pltpu.make_async_copy(
                table_ref.at[pl.ds(c * size, size)], held.at[pl.ds(c * size, size)], in_sems.at[c]
            )
            for c in range(chunks)
        ]
        stores = [
            pltpu.make_async_copy(joined.at[user], out_ref.at[user], out_sems.at[user])
            for user in range(users)
        ]
        indices = pltpu.make_async_copy(places_ref, near, near_sem)
        for load in loads:
            load.start()
        indices.start()
        for c in range(chunks):
            loads[c].wait()
            spread_rows(held, wide, c * size, size)
        indices.wait()
        for user in range(users):

            @pl.loop(0, count // unroll)
            def _(i):
                for u in range(unroll):
                    o = i * unroll + u
                    pick_row(near[user * stride + o], wide, picked, user * count + o, parts)

            join_rows(picked, joined.at[user], user * count, count, parts)
            stores[user].start()
        for store in stores:
            store.wait()

    return pl.pallas_call(
        kernel,
        out_shape=jax.ShapeDtypeStruct((users, count, width), BF16),
        in_specs=[ANY, ANY],
        out_specs=ANY,
        scratch_shapes=[
            pltpu.SMEM((users * stride,), jnp.int32),
            pltpu.VMEM((rows, width), BF16),
            pltpu.VMEM((rows * parts, LANES), F32),
            pltpu.VMEM((users * count * parts, LANES), F32),
            pltpu.VMEM((users, count, width), BF16),
            pltpu.SemaphoreType.DMA,
            pltpu.SemaphoreType.DMA((chunks,)),
            pltpu.SemaphoreType.DMA((users,)),
        ],
        compiler_params=pltpu.CompilerParams(vmem_limit_bytes=62 * MIB),
        name="gather_rows",
    )(places, table)


def project_rows(fetched, places, w_uvqk):
    count, width = fetched.shape
    tokens = places.shape[0]
    parts = width // LANES
    half = tokens // 2
    tiles = tokens // TILE

    def kernel(places_ref, rows_ref, w_in, low_ref, high_ref, act, wide, picked, w_ref, sem):
        load = pltpu.make_async_copy(w_in, w_ref, sem)
        load.start()
        spread_rows(rows_ref, wide, 0, count)

        def pick_tile(t):
            for j in range(t * TILE, (t + 1) * TILE):
                pick_row(places_ref[j], wide, picked, j, parts)

        pick_tile(0)
        load.wait()
        for t in range(tiles):
            if t + 1 < tiles:
                pick_tile(t + 1)
            row = t * TILE
            events = jnp.concatenate(
                [picked[pl.ds(parts * row + k, TILE, stride=parts), :] for k in range(parts)], axis=1
            )
            target = low_ref if row < half else high_ref
            target[row % half : row % half + TILE, :] = events.astype(BF16)
            normed = normalize(events, 0.5).astype(BF16)
            for k in range(4):
                cols = slice(k * width, (k + 1) * width)
                act[row : row + TILE, cols] = silu_of_twice(dot(normed, w_ref[:, cols])).astype(BF16)

    out = jax.ShapeDtypeStruct((half, width), BF16)
    return pl.pallas_call(
        kernel,
        out_shape=(out, out, jax.ShapeDtypeStruct((tokens, 4 * width), BF16)),
        in_specs=[SMEM, VMEM, HBM],
        out_specs=(VMEM, VMEM, VMEM),
        scratch_shapes=[
            pltpu.VMEM((count * parts, LANES), F32),
            pltpu.VMEM((tokens * parts, LANES), F32),
            pltpu.VMEM((width, 4 * width), BF16),
            pltpu.SemaphoreType.DMA,
        ],
        compiler_params=pltpu.CompilerParams(vmem_limit_bytes=32 * MIB),
        name="project_rows",
    )(places, fetched, pltpu.with_memory_space_constraint(w_uvqk, pltpu.HBM))


def lower_mask():
    row = lax.broadcasted_iota(jnp.int32, (TILE, TILE), 0)
    column = lax.broadcasted_iota(jnp.int32, (TILE, TILE), 1)
    return column <= row


def finish(attended, gate, events, w_out, limit, first):
    gated = (normalize(attended) * gate.astype(F32)).astype(BF16)
    result = dot(gated, w_out) + events.astype(F32)
    position = first + lax.broadcasted_iota(jnp.int32, result.shape, 0)
    return jnp.where(position < limit, result, 0.0).astype(BF16)


def own_part(limit, act, high, w_out):
    half, width = high.shape
    tokens = 2 * half
    head = width // HEADS
    scale = head ** (-0.5)
    reach = WINDOW // TILE
    tiles = tokens // TILE

    def kernel(limit_ref, act, high_ref, wo_ref, out_ref, part_ref, done, sem):
        mask = lower_mask()

        def cols_of(k, h):
            return slice(k * width + h * head, k * width + (h + 1) * head)

        for t in range(reach):
            rows = slice(t * TILE, (t + 1) * TILE)
            for h in range(HEADS):
                query = act[rows, cols_of(1, h)]
                scores = dot_nt(query, act[0 : (t + 1) * TILE, cols_of(2, h)])
                weights = silu_of_twice(scores * (0.5 * scale))
                diagonal = jnp.where(mask, weights[:, t * TILE :], 0.0).astype(BF16)
                total = dot(diagonal, act[rows, cols_of(3, h)])
                if t:
                    total += dot(weights[:, : t * TILE].astype(BF16), act[0 : t * TILE, cols_of(3, h)])
                part_ref[rows, h * head : (h + 1) * head] = total

        @pl.loop(0, tiles - reach, unroll=True)
        def _(i):
            t = i + reach
            row = pl.multiple_of(t * TILE, TILE)
            back = pl.multiple_of(i * TILE, TILE)
            pieces = []
            for h in range(HEADS):
                query = act[pl.ds(row, TILE), cols_of(1, h)]
                edge = dot_nt(query, act[pl.ds(back, TILE), cols_of(2, h)])
                inner = dot_nt(query, act[pl.ds(back + TILE, WINDOW - TILE), cols_of(2, h)])
                last = dot_nt(query, act[pl.ds(row, TILE), cols_of(2, h)])
                both = silu_of_twice(jnp.where(mask, last, edge) * (0.5 * scale))
                total = dot(
                    silu_of_twice(inner * (0.5 * scale)).astype(BF16),
                    act[pl.ds(back + TILE, WINDOW - TILE), cols_of(3, h)],
                )
                total += dot(
                    jnp.where(mask, both, 0.0).astype(BF16), act[pl.ds(row, TILE), cols_of(3, h)]
                )
                total += dot(
                    jnp.where(mask, 0.0, both).astype(BF16), act[pl.ds(back, TILE), cols_of(3, h)]
                )
                pieces.append(total)
            done[pl.ds(back, TILE), :] = finish(
                jnp.concatenate(pieces, axis=1),
                act[pl.ds(row, TILE), 0:width],
                high_ref[pl.ds(back, TILE), :],
                wo_ref[...],
                limit_ref[0],
                row,
            )

        copy = pltpu.make_async_copy(done, out_ref.at[pl.ds(half, half)], sem)
        copy.start()
        copy.wait()

    return pl.pallas_call(
        kernel,
        out_shape=(
            jax.ShapeDtypeStruct((tokens, width), BF16),
            jax.ShapeDtypeStruct((half, width), F32),
        ),
        in_specs=[SMEM, VMEM, VMEM, VMEM],
        out_specs=(ANY, VMEM),
        scratch_shapes=[
            pltpu.VMEM((half, width), BF16),
            pltpu.SemaphoreType.DMA,
        ],
        compiler_params=pltpu.CompilerParams(vmem_limit_bytes=20 * MIB),
        cost_estimate=pl.CostEstimate(
            flops=14_000_000_000, bytes_accessed=12_000_000, transcendentals=12_000_000
        ),
        name="own_part",
    )(limit, act, high, w_out)


def halo_part(limit, before, part, act, low, w_uvqk, w_out, out):
    half, width = low.shape
    head = width // HEADS
    reach = WINDOW // TILE

    def kernel(
        limit_ref, before_ref, part_ref, act, low_ref, w_ref, wo_ref, _, out_ref, keyvals, done, sem
    ):
        @pl.loop(0, half // TILE, unroll=True)
        def _(i):
            row = pl.multiple_of(i * TILE, TILE)
            normed = normalize(before_ref[pl.ds(row, TILE), :].astype(F32), 0.5).astype(BF16)
            for k in range(2):
                cols = slice((k + 2) * width, (k + 3) * width)
                keyvals[pl.ds(row, TILE), k * width : (k + 1) * width] = silu_of_twice(
                    dot(normed, w_ref[:, cols])
                ).astype(BF16)

        mask = lower_mask()
        for t in range(reach):
            rows = slice(t * TILE, (t + 1) * TILE)
            pieces = []
            for h in range(HEADS):
                cols = slice(h * head, (h + 1) * head)
                vcols = slice(width + h * head, width + (h + 1) * head)
                weights = silu_of_twice(dot_nt(act[rows, width + h * head : width + (h + 1) * head], keyvals[t * TILE :, cols]) * (0.5 * head ** (-0.5)))
                edge = jnp.where(mask, 0.0, weights[:, :TILE]).astype(BF16)
                total = part_ref[rows, cols] + dot(edge, keyvals[rows, vcols])
                if t + 1 < reach:
                    total += dot(weights[:, TILE:].astype(BF16), keyvals[(t + 1) * TILE :, vcols])
                pieces.append(total)
            done[rows, :] = finish(
                jnp.concatenate(pieces, axis=1),
                act[rows, 0:width],
                low_ref[rows, :],
                wo_ref[...],
                limit_ref[0],
                t * TILE,
            )
        copy = pltpu.make_async_copy(done, out_ref.at[pl.ds(0, half)], sem)
        copy.start()
        copy.wait()

    return pl.pallas_call(
        kernel,
        out_shape=jax.ShapeDtypeStruct(out.shape, out.dtype),
        in_specs=[SMEM, VMEM, VMEM, VMEM, VMEM, VMEM, VMEM, ANY],
        out_specs=ANY,
        scratch_shapes=[
            pltpu.VMEM((half, 2 * width), BF16),
            pltpu.VMEM((half, width), BF16),
            pltpu.SemaphoreType.DMA,
        ],
        input_output_aliases={7: 0},
        compiler_params=pltpu.CompilerParams(vmem_limit_bytes=20 * MIB),
        name="halo_part",
    )(limit, before, part, act, low, w_uvqk, w_out, out)


def local(embed_table, lookup_ids, counts, event_order, hist_len, w_uvqk, w_out):
    shards = lax.axis_size("table")
    capacity = lookup_ids.shape[3]
    tokens = event_order.shape[2]
    width = embed_table.shape[1]
    parts = width // LANES
    exchange = lambda rows: lax.all_to_all(rows, "table", split_axis=0, concat_axis=0, tiled=True)
    stride = -(-capacity // LANES) * LANES
    starts_in_wide = jnp.pad(parts * lookup_ids[0, 0], ((0, 0), (0, stride - capacity)))
    requests = exchange(starts_in_wide.reshape(shards, stride // LANES, LANES)).reshape(shards * stride)
    fetched = exchange(gather_rows(embed_table, requests, shards, capacity, stride))
    live_counts = counts[0, 0]
    totals = jnp.cumsum(live_counts)
    starts = totals - live_counts
    event_rank = event_order[0, 0]
    owner_shard = jnp.sum((event_rank[:, None] >= totals[None, :]).astype(jnp.int32), axis=1)
    chosen = owner_shard[:, None] == jnp.arange(shards, dtype=jnp.int32)[None, :]
    slot_start = jnp.sum(jnp.where(chosen, starts[None, :], 0), axis=1)
    place = owner_shard * capacity + event_rank - slot_start
    low, high, act = project_rows(fetched.reshape(shards * capacity, width), parts * place, w_uvqk)
    before = passed_along(high, "seq", 1)
    limit = hist_len - lax.axis_index("seq") * tokens
    out, part = own_part(limit, act, high, w_out)
    result = halo_part(limit, before, part, act, low, w_uvqk, w_out, out)
    return result[None]


def solution(mesh):
    in_specs = (
        P("table", None),
        P("table", "seq", None, None),
        P("table", "seq", None),
        P("table", "seq", None),
        P("table"),
        P(),
        P(),
    )
    out_specs = P("table", "seq", None)
    return jax.shard_map(local, mesh=mesh, in_specs=in_specs, out_specs=out_specs, check_vma=False)
```

```python
import jax
import jax.numpy as jnp
from jax import lax
from jax.experimental import pallas as pl
from jax.experimental.pallas import tpu as pltpu
from jax.sharding import PartitionSpec as P

HEADS = 4
WINDOW = 1024
TILE = 256
LANES = 128
MIB = 1 << 20
F32 = jnp.float32
BF16 = jnp.bfloat16
VMEM = pl.BlockSpec(memory_space=pltpu.VMEM)
SMEM = pl.BlockSpec(memory_space=pltpu.SMEM)
ANY = pl.BlockSpec(memory_space=pl.ANY)
HBM = pl.BlockSpec(memory_space=pltpu.HBM)


def passed_along(value, axis, steps):
    count = lax.axis_size(axis)
    initial, last = (max(0, -steps), min(count, count - steps))
    return lax.ppermute(value, axis, [(source, source + steps) for source in range(initial, last)])


def normalize(values, factor=1.0):
    average = jnp.mean(values, axis=-1, keepdims=True)
    centered = values - average
    spread = jnp.mean(centered * centered, axis=-1, keepdims=True)
    return centered * (factor * lax.rsqrt(spread + 1e-05))


def silu_of_twice(half):
    return half + half * jnp.tanh(half)


def dot(a, b):
    return jnp.dot(a, b, preferred_element_type=F32)


def dot_nt(a, b):
    return lax.dot_general(a, b, (((1,), (1,)), ((), ())), preferred_element_type=F32)


def spread_rows(source, target, first, count, base=0):
    step = 32
    parts = source.shape[1] // LANES

    @pl.loop(0, count // step)
    def _(i):
        row = pl.multiple_of(first + i * step, step)
        block = source[pl.ds(row, step), :].astype(F32)
        for k in range(parts):
            target[pl.ds(parts * (base + row) + k, step, stride=parts), :] = block[
                :, k * LANES : (k + 1) * LANES
            ]


def pick_row(place, source, target, j, parts):
    target[pl.ds(pl.multiple_of(parts * j, parts), parts), :] = source[
        pl.ds(pl.multiple_of(place, parts), parts), :
    ]


def join_rows(source, target, first, count, parts):
    step = 32

    @pl.loop(0, count // step)
    def _(i):
        row = pl.multiple_of(i * step, step)
        for k in range(parts):
            target[pl.ds(row, step), k * LANES : (k + 1) * LANES] = source[
                pl.ds(parts * (first + row) + k, step, stride=parts), :
            ].astype(BF16)


def gather_rows(table, places, users, count, stride):
    rows, width = table.shape
    parts = width // LANES
    chunks = 8
    size = rows // chunks
    unroll = 32 if count % 32 == 0 else 16

    def kernel(places_ref, table_ref, out_ref, near, held, wide, picked, joined, near_sem, in_sems, out_sems):
        loads = [
            pltpu.make_async_copy(
                table_ref.at[pl.ds(c * size, size)], held.at[pl.ds(c * size, size)], in_sems.at[c]
            )
            for c in range(chunks)
        ]
        stores = [
            pltpu.make_async_copy(joined.at[user], out_ref.at[user], out_sems.at[user])
            for user in range(users)
        ]
        indices = pltpu.make_async_copy(places_ref, near, near_sem)
        for load in loads:
            load.start()
        indices.start()
        for c in range(chunks):
            loads[c].wait()
            spread_rows(held, wide, c * size, size)
        indices.wait()
        for user in range(users):

            @pl.loop(0, count // unroll)
            def _(i):
                for u in range(unroll):
                    o = i * unroll + u
                    pick_row(near[user * stride + o], wide, picked, user * count + o, parts)

            join_rows(picked, joined.at[user], user * count, count, parts)
            stores[user].start()
        for store in stores:
            store.wait()

    return pl.pallas_call(
        kernel,
        out_shape=jax.ShapeDtypeStruct((users, count, width), BF16),
        in_specs=[ANY, ANY],
        out_specs=ANY,
        scratch_shapes=[
            pltpu.SMEM((users * stride,), jnp.int32),
            pltpu.VMEM((rows, width), BF16),
            pltpu.VMEM((rows * parts, LANES), F32),
            pltpu.VMEM((users * count * parts, LANES), F32),
            pltpu.VMEM((users, count, width), BF16),
            pltpu.SemaphoreType.DMA,
            pltpu.SemaphoreType.DMA((chunks,)),
            pltpu.SemaphoreType.DMA((users,)),
        ],
        compiler_params=pltpu.CompilerParams(vmem_limit_bytes=62 * MIB),
        name="gather_rows",
    )(places, table)


def project_rows(fetched, places, w_uvqk):
    count, width = fetched.shape
    tokens = places.shape[0]
    parts = width // LANES
    half = tokens // 2
    tiles = tokens // TILE

    def kernel(places_ref, rows_ref, w_in, low_ref, high_ref, act, wide, picked, w_ref, sem):
        load = pltpu.make_async_copy(w_in, w_ref, sem)
        load.start()
        spread_rows(rows_ref, wide, 0, count)

        def pick_tile(t):
            for j in range(t * TILE, (t + 1) * TILE):
                pick_row(places_ref[j], wide, picked, j, parts)

        pick_tile(0)
        load.wait()
        for t in range(tiles):
            if t + 1 < tiles:
                pick_tile(t + 1)
            row = t * TILE
            events = jnp.concatenate(
                [picked[pl.ds(parts * row + k, TILE, stride=parts), :] for k in range(parts)], axis=1
            )
            target = low_ref if row < half else high_ref
            target[row % half : row % half + TILE, :] = events.astype(BF16)
            normed = normalize(events, 0.5).astype(BF16)
            for k in range(4):
                cols = slice(k * width, (k + 1) * width)
                act[row : row + TILE, cols] = silu_of_twice(dot(normed, w_ref[:, cols])).astype(BF16)

    out = jax.ShapeDtypeStruct((half, width), BF16)
    return pl.pallas_call(
        kernel,
        out_shape=(out, out, jax.ShapeDtypeStruct((tokens, 4 * width), BF16)),
        in_specs=[SMEM, VMEM, HBM],
        out_specs=(VMEM, VMEM, VMEM),
        scratch_shapes=[
            pltpu.VMEM((count * parts, LANES), F32),
            pltpu.VMEM((tokens * parts, LANES), F32),
            pltpu.VMEM((width, 4 * width), BF16),
            pltpu.SemaphoreType.DMA,
        ],
        compiler_params=pltpu.CompilerParams(vmem_limit_bytes=32 * MIB),
        name="project_rows",
    )(places, fetched, pltpu.with_memory_space_constraint(w_uvqk, pltpu.HBM))


def lower_mask():
    row = lax.broadcasted_iota(jnp.int32, (TILE, TILE), 0)
    column = lax.broadcasted_iota(jnp.int32, (TILE, TILE), 1)
    return column <= row


def finish(attended, gate, events, w_out, limit, first):
    gated = (normalize(attended) * gate.astype(F32)).astype(BF16)
    result = dot(gated, w_out) + events.astype(F32)
    position = first + lax.broadcasted_iota(jnp.int32, result.shape, 0)
    return jnp.where(position < limit, result, 0.0).astype(BF16)


def own_part(limit, act, high, w_out):
    half, width = high.shape
    tokens = 2 * half
    head = width // HEADS
    scale = head ** (-0.5)
    reach = WINDOW // TILE
    tiles = tokens // TILE

    def kernel(limit_ref, act, high_ref, wo_ref, out_ref, part_ref, done, held, sums, sems):
        stores = [
            pltpu.make_async_copy(
                done.at[pl.ds(i * TILE, TILE)], out_ref.at[pl.ds(half + i * TILE, TILE)], sems.at[i]
            )
            for i in range(tiles - reach)
        ]
        mask = lower_mask()

        def cols_of(k, h):
            return slice(k * width + h * head, k * width + (h + 1) * head)

        def weigh(m, h, slot):
            key = act[m * TILE : (m + 1) * TILE, cols_of(2, h)]
            count = min(reach, tiles - m)
            scores = dot_nt(act[m * TILE : (m + count) * TILE, cols_of(1, h)], key)
            near = scores[:TILE]
            if m >= reach:
                far = act[(m - reach) * TILE : (m - reach + 1) * TILE, cols_of(2, h)]
                near = jnp.where(mask, near, dot_nt(act[m * TILE : (m + 1) * TILE, cols_of(1, h)], far))
            near = silu_of_twice(near * (0.5 * scale))
            held[slot, 0:TILE, :] = jnp.where(mask, near, 0.0).astype(BF16)
            if m >= reach:
                held[slot, reach * TILE :, :] = jnp.where(mask, 0.0, near).astype(BF16)
            if count > 1:
                held[slot, TILE : count * TILE, :] = silu_of_twice(scores[TILE:] * (0.5 * scale)).astype(BF16)

        def attend(m, h, slot):
            cols = slice(h * head, (h + 1) * head)
            count = min(reach, tiles - m)
            added = dot(held[slot, : count * TILE, :], act[m * TILE : (m + 1) * TILE, cols_of(3, h)])
            for i in range(count):
                rows = slice((m + i) * TILE, (m + i + 1) * TILE)
                more = added[i * TILE : (i + 1) * TILE]
                if i == 0 and m >= reach:
                    far = act[(m - reach) * TILE : (m - reach + 1) * TILE, cols_of(3, h)]
                    more += dot(held[slot, reach * TILE :, :], far)
                sums[rows, cols] = more if m == 0 or i == reach - 1 else sums[rows, cols] + more

        units = [(m, h) for m in range(tiles) for h in range(HEADS)]
        for u in range(len(units) + 1):
            if u < len(units):
                weigh(*units[u], u % 2)
            if u == 0:
                continue
            m, h = units[u - 1]
            attend(m, h, (u - 1) % 2)
            if h + 1 < HEADS:
                continue
            rows = slice(m * TILE, (m + 1) * TILE)
            if m < reach:
                part_ref[rows, :] = sums[rows, :]
            else:
                back = slice((m - reach) * TILE, (m - reach + 1) * TILE)
                done[back, :] = finish(
                    sums[rows, :], act[rows, 0:width], high_ref[back, :], wo_ref[...], limit_ref[0], m * TILE
                )
                stores[m - reach].start()

        for store in stores:
            store.wait()

    return pl.pallas_call(
        kernel,
        out_shape=(
            jax.ShapeDtypeStruct((tokens, width), BF16),
            jax.ShapeDtypeStruct((half, width), F32),
        ),
        in_specs=[SMEM, VMEM, VMEM, VMEM],
        out_specs=(ANY, VMEM),
        scratch_shapes=[
            pltpu.VMEM((half, width), BF16),
            pltpu.VMEM((2, WINDOW + TILE, TILE), BF16),
            pltpu.VMEM((tokens, width), F32),
            pltpu.SemaphoreType.DMA((tiles - reach,)),
        ],
        compiler_params=pltpu.CompilerParams(vmem_limit_bytes=20 * MIB),
        cost_estimate=pl.CostEstimate(
            flops=14_000_000_000, bytes_accessed=12_000_000, transcendentals=12_000_000
        ),
        name="own_part",
    )(limit, act, high, w_out)


def halo_part(limit, before, part, act, low, w_uvqk, w_out, out):
    half, width = low.shape
    head = width // HEADS
    scale = head ** (-0.5)
    reach = WINDOW // TILE

    def kernel(
        limit_ref, before_ref, part_ref, act, low_ref, w_in, wo_ref, _, out_ref, keyvals, done, w_ref, held, sums, sems
    ):
        stores = [
            pltpu.make_async_copy(
                done.at[pl.ds(i * TILE, TILE)], out_ref.at[pl.ds(i * TILE, TILE)], sems.at[i]
            )
            for i in range(reach)
        ]
        w_ref[...] = w_in[:, 2 * width :]
        mask = lower_mask()

        def project(m):
            rows = slice(m * TILE, (m + 1) * TILE)
            normed = normalize(before_ref[rows, :].astype(F32), 0.5).astype(BF16)
            for k in range(2):
                cols = slice(k * width, (k + 1) * width)
                keyvals[rows, cols] = silu_of_twice(dot(normed, w_ref[:, cols])).astype(BF16)

        def weigh(m, h, slot):
            scores = dot_nt(
                act[0 : (m + 1) * TILE, width + h * head : width + (h + 1) * head],
                keyvals[m * TILE : (m + 1) * TILE, h * head : (h + 1) * head],
            )
            weights = silu_of_twice(scores * (0.5 * scale))
            if m:
                held[slot, 0 : m * TILE, :] = weights[: m * TILE].astype(BF16)
            held[slot, m * TILE : (m + 1) * TILE, :] = jnp.where(mask, 0.0, weights[m * TILE :]).astype(BF16)

        def attend(m, h, slot):
            cols = slice(h * head, (h + 1) * head)
            rows = slice(0, (m + 1) * TILE)
            values = keyvals[m * TILE : (m + 1) * TILE, width + h * head : width + (h + 1) * head]
            so_far = part_ref if m + 1 == reach else sums
            sums[rows, cols] = so_far[rows, cols] + dot(held[slot, rows, :], values)

        units = [(m, h) for m in reversed(range(reach)) for h in range(HEADS)]
        for m in reversed(range(reach)):
            project(m)
        for u in range(len(units) + 1):
            if u < len(units):
                weigh(*units[u], u % 2)
            if u == 0:
                continue
            m, h = units[u - 1]
            attend(m, h, (u - 1) % 2)
            if h + 1 < HEADS:
                continue
            rows = slice(m * TILE, (m + 1) * TILE)
            done[rows, :] = finish(
                sums[rows, :], act[rows, 0:width], low_ref[rows, :], wo_ref[...], limit_ref[0], m * TILE
            )
            stores[m].start()
        for store in stores:
            store.wait()

    return pl.pallas_call(
        kernel,
        out_shape=jax.ShapeDtypeStruct(out.shape, out.dtype),
        in_specs=[SMEM, VMEM, VMEM, VMEM, VMEM, VMEM, VMEM, ANY],
        out_specs=ANY,
        scratch_shapes=[
            pltpu.VMEM((half, 2 * width), BF16),
            pltpu.VMEM((half, width), BF16),
            pltpu.VMEM((width, 2 * width), BF16),
            pltpu.VMEM((2, WINDOW, TILE), BF16),
            pltpu.VMEM((half, width), F32),
            pltpu.SemaphoreType.DMA((reach,)),
        ],
        input_output_aliases={7: 0},
        compiler_params=pltpu.CompilerParams(vmem_limit_bytes=20 * MIB),
        name="halo_part",
    )(limit, before, part, act, low, w_uvqk, w_out, out)


def local(embed_table, lookup_ids, counts, event_order, hist_len, w_uvqk, w_out):
    shards = lax.axis_size("table")
    capacity = lookup_ids.shape[3]
    tokens = event_order.shape[2]
    width = embed_table.shape[1]
    parts = width // LANES
    exchange = lambda rows: lax.all_to_all(rows, "table", split_axis=0, concat_axis=0, tiled=True)
    stride = -(-capacity // LANES) * LANES
    starts_in_wide = jnp.pad(parts * lookup_ids[0, 0], ((0, 0), (0, stride - capacity)))
    requests = exchange(starts_in_wide.reshape(shards, stride // LANES, LANES)).reshape(shards * stride)
    fetched = exchange(gather_rows(embed_table, requests, shards, capacity, stride))
    live_counts = counts[0, 0]
    totals = jnp.cumsum(live_counts)
    starts = totals - live_counts
    event_rank = event_order[0, 0]
    owner_shard = jnp.sum((event_rank[:, None] >= totals[None, :]).astype(jnp.int32), axis=1)
    chosen = owner_shard[:, None] == jnp.arange(shards, dtype=jnp.int32)[None, :]
    slot_start = jnp.sum(jnp.where(chosen, starts[None, :], 0), axis=1)
    place = owner_shard * capacity + event_rank - slot_start
    low, high, act = project_rows(fetched.reshape(shards * capacity, width), parts * place, w_uvqk)
    before = passed_along(high, "seq", 1)
    limit = hist_len - lax.axis_index("seq") * tokens
    out, part = own_part(limit, act, high, w_out)
    result = halo_part(limit, before, part, act, low, w_uvqk, w_out, out)
    return result[None]


def solution(mesh):
    in_specs = (
        P("table", None),
        P("table", "seq", None, None),
        P("table", "seq", None),
        P("table", "seq", None),
        P("table"),
        P(),
        P(),
    )
    out_specs = P("table", "seq", None)
    return jax.shard_map(local, mesh=mesh, in_specs=in_specs, out_specs=out_specs, check_vma=False)
```

```python
import jax
import jax.numpy as jnp
from jax import lax
from jax.experimental import pallas as pl
from jax.experimental.pallas import tpu as pltpu
from jax.sharding import PartitionSpec as P

HEADS = 4
WINDOW = 1024
TILE = 256
LANES = 128
MIB = 1 << 20
F32 = jnp.float32
BF16 = jnp.bfloat16
VMEM = pl.BlockSpec(memory_space=pltpu.VMEM)
SMEM = pl.BlockSpec(memory_space=pltpu.SMEM)
ANY = pl.BlockSpec(memory_space=pl.ANY)
HBM = pl.BlockSpec(memory_space=pltpu.HBM)


def passed_along(value, axis, steps):
    count = lax.axis_size(axis)
    initial, last = (max(0, -steps), min(count, count - steps))
    return lax.ppermute(value, axis, [(source, source + steps) for source in range(initial, last)])


def normalize(values, factor=1.0):
    average = jnp.mean(values, axis=-1, keepdims=True)
    centered = values - average
    spread = jnp.mean(centered * centered, axis=-1, keepdims=True)
    return centered * (factor * lax.rsqrt(spread + 1e-05))


def silu_of_twice(half):
    return half + half * jnp.tanh(half)


def dot(a, b):
    return jnp.dot(a, b, preferred_element_type=F32)


def dot_nt(a, b):
    return lax.dot_general(a, b, (((1,), (1,)), ((), ())), preferred_element_type=F32)


def spread_rows(source, target, first, count, base=0):
    step = 64
    parts = source.shape[1] // LANES

    @pl.loop(0, count // step)
    def _(i):
        row = pl.multiple_of(first + i * step, step)
        block = source[pl.ds(row, step), :].astype(F32)
        for k in range(parts):
            target[pl.ds(parts * (base + row) + k, step, stride=parts), :] = block[
                :, k * LANES : (k + 1) * LANES
            ]


def pick_row(place, source, target, j, parts):
    target[pl.ds(pl.multiple_of(parts * j, parts), parts), :] = source[
        pl.ds(pl.multiple_of(place, parts), parts), :
    ]


def join_rows(source, target, first, count, parts):
    step = 32

    @pl.loop(0, count // step)
    def _(i):
        row = pl.multiple_of(i * step, step)
        for k in range(parts):
            target[pl.ds(row, step), k * LANES : (k + 1) * LANES] = source[
                pl.ds(parts * (first + row) + k, step, stride=parts), :
            ].astype(BF16)


def gather_rows(table, places, users, count, stride):
    rows, width = table.shape
    parts = width // LANES
    chunks = 16
    size = rows // chunks
    unroll = 32 if count % 32 == 0 else 16

    def kernel(places_ref, table_ref, out_ref, near, held, wide, picked, joined, near_sem, in_sems, out_sems):
        loads = [
            pltpu.make_async_copy(
                table_ref.at[pl.ds(c * size, size)], held.at[pl.ds(c * size, size)], in_sems.at[c]
            )
            for c in range(chunks)
        ]
        stores = [
            pltpu.make_async_copy(joined.at[user], out_ref.at[user], out_sems.at[user])
            for user in range(users)
        ]
        indices = pltpu.make_async_copy(places_ref, near, near_sem)
        for load in loads:
            load.start()
        indices.start()
        for c in range(chunks):
            loads[c].wait()
            spread_rows(held, wide, c * size, size)
        indices.wait()
        def pick(user):
            for o in range(count):
                pick_row(near[user * stride + o], wide, picked, user * count + o, parts)

        def join(user):
            for k in range(parts):
                joined[user, :, k * LANES : (k + 1) * LANES] = picked[
                    pl.ds(parts * user * count + k, count, stride=parts), :
                ].astype(BF16)
            pltpu.make_async_copy(joined.at[user], out_ref.at[user], out_sems.at[user]).start()

        pick(0)

        @pl.loop(1, users)
        def _(user):
            pick(user)
            join(user - 1)

        join(users - 1)
        for store in stores:
            store.wait()

    return pl.pallas_call(
        kernel,
        out_shape=jax.ShapeDtypeStruct((users, count, width), BF16),
        in_specs=[ANY, ANY],
        out_specs=ANY,
        scratch_shapes=[
            pltpu.SMEM((users * stride,), jnp.int32),
            pltpu.VMEM((rows, width), BF16),
            pltpu.VMEM((rows * parts, LANES), F32),
            pltpu.VMEM((users * count * parts, LANES), F32),
            pltpu.VMEM((users, count, width), BF16),
            pltpu.SemaphoreType.DMA,
            pltpu.SemaphoreType.DMA((chunks,)),
            pltpu.SemaphoreType.DMA((users,)),
        ],
        compiler_params=pltpu.CompilerParams(vmem_limit_bytes=62 * MIB),
        name="gather_rows",
    )(places, table)


def project_rows(fetched, places, w_uvqk):
    count, width = fetched.shape
    tokens = places.shape[0]
    parts = width // LANES
    half = tokens // 2
    tiles = tokens // TILE

    def kernel(places_ref, rows_ref, w_in, low_ref, high_ref, act, wide, picked, w_ref, sem):
        load = pltpu.make_async_copy(w_in, w_ref, sem)
        load.start()
        spread_rows(rows_ref, wide, 0, count)

        def pick_tile(t):
            for j in range(t * TILE, (t + 1) * TILE):
                pick_row(places_ref[j], wide, picked, j, parts)

        pick_tile(0)
        load.wait()
        for t in range(tiles):
            if t + 1 < tiles:
                pick_tile(t + 1)
            row = t * TILE
            events = jnp.concatenate(
                [picked[pl.ds(parts * row + k, TILE, stride=parts), :] for k in range(parts)], axis=1
            )
            target = low_ref if row < half else high_ref
            target[row % half : row % half + TILE, :] = events.astype(BF16)
            normed = normalize(events, 0.5).astype(BF16)
            for k in range(4):
                cols = slice(k * width, (k + 1) * width)
                act[row : row + TILE, cols] = silu_of_twice(dot(normed, w_ref[:, cols])).astype(BF16)

    out = jax.ShapeDtypeStruct((half, width), BF16)
    return pl.pallas_call(
        kernel,
        out_shape=(out, out, jax.ShapeDtypeStruct((tokens, 4 * width), BF16)),
        in_specs=[SMEM, VMEM, HBM],
        out_specs=(VMEM, VMEM, VMEM),
        scratch_shapes=[
            pltpu.VMEM((count * parts, LANES), F32),
            pltpu.VMEM((tokens * parts, LANES), F32),
            pltpu.VMEM((width, 4 * width), BF16),
            pltpu.SemaphoreType.DMA,
        ],
        compiler_params=pltpu.CompilerParams(vmem_limit_bytes=32 * MIB),
        name="project_rows",
    )(places, fetched, pltpu.with_memory_space_constraint(w_uvqk, pltpu.HBM))


def lower_mask():
    row = lax.broadcasted_iota(jnp.int32, (TILE, TILE), 0)
    column = lax.broadcasted_iota(jnp.int32, (TILE, TILE), 1)
    return column <= row


def finish(attended, gate, events, w_out, limit, first):
    gated = (normalize(attended) * gate.astype(F32)).astype(BF16)
    result = dot(gated, w_out) + events.astype(F32)
    position = first + lax.broadcasted_iota(jnp.int32, result.shape, 0)
    return jnp.where(position < limit, result, 0.0).astype(BF16)


def own_part(limit, act, high, w_out):
    half, width = high.shape
    tokens = 2 * half
    head = width // HEADS
    scale = head ** (-0.5)
    reach = WINDOW // TILE
    tiles = tokens // TILE

    def kernel(limit_ref, act, high_ref, wo_ref, out_ref, part_ref, done, held, sums, sems):
        stores = [
            pltpu.make_async_copy(
                done.at[pl.ds(i * TILE, TILE)], out_ref.at[pl.ds(half + i * TILE, TILE)], sems.at[i]
            )
            for i in range(tiles - reach)
        ]
        mask = lower_mask()

        def cols_of(k, h):
            return slice(k * width + h * head, k * width + (h + 1) * head)

        def weigh(m, h, slot):
            key = act[m * TILE : (m + 1) * TILE, cols_of(2, h)]
            count = min(reach, tiles - m)
            scores = dot_nt(act[m * TILE : (m + count) * TILE, cols_of(1, h)], key)
            near = scores[:TILE]
            if m >= reach:
                far = act[(m - reach) * TILE : (m - reach + 1) * TILE, cols_of(2, h)]
                near = jnp.where(mask, near, dot_nt(act[m * TILE : (m + 1) * TILE, cols_of(1, h)], far))
            near = silu_of_twice(near * (0.5 * scale))
            held[slot, 0:TILE, :] = jnp.where(mask, near, 0.0).astype(BF16)
            if m >= reach:
                held[slot, reach * TILE :, :] = jnp.where(mask, 0.0, near).astype(BF16)
            if count > 1:
                held[slot, TILE : count * TILE, :] = silu_of_twice(scores[TILE:] * (0.5 * scale)).astype(BF16)

        def attend(m, h, slot):
            cols = slice(h * head, (h + 1) * head)
            count = min(reach, tiles - m)
            added = dot(held[slot, : count * TILE, :], act[m * TILE : (m + 1) * TILE, cols_of(3, h)])
            for i in range(count):
                rows = slice((m + i) * TILE, (m + i + 1) * TILE)
                more = added[i * TILE : (i + 1) * TILE]
                if i == 0 and m >= reach:
                    far = act[(m - reach) * TILE : (m - reach + 1) * TILE, cols_of(3, h)]
                    more += dot(held[slot, reach * TILE :, :], far)
                sums[rows, cols] = more if m == 0 or i == reach - 1 else sums[rows, cols] + more

        units = [(m, h) for m in range(tiles) for h in range(HEADS)]
        for u in range(len(units) + 1):
            if u < len(units):
                weigh(*units[u], u % 2)
            if u == 0:
                continue
            m, h = units[u - 1]
            attend(m, h, (u - 1) % 2)
            if h + 1 < HEADS:
                continue
            rows = slice(m * TILE, (m + 1) * TILE)
            if m < reach:
                part_ref[rows, :] = sums[rows, :]
            else:
                back = slice((m - reach) * TILE, (m - reach + 1) * TILE)
                done[back, :] = finish(
                    sums[rows, :], act[rows, 0:width], high_ref[back, :], wo_ref[...], limit_ref[0], m * TILE
                )
                stores[m - reach].start()

        for store in stores:
            store.wait()

    return pl.pallas_call(
        kernel,
        out_shape=(
            jax.ShapeDtypeStruct((tokens, width), BF16),
            jax.ShapeDtypeStruct((half, width), F32),
        ),
        in_specs=[SMEM, VMEM, VMEM, VMEM],
        out_specs=(ANY, VMEM),
        scratch_shapes=[
            pltpu.VMEM((half, width), BF16),
            pltpu.VMEM((2, WINDOW + TILE, TILE), BF16),
            pltpu.VMEM((tokens, width), F32),
            pltpu.SemaphoreType.DMA((tiles - reach,)),
        ],
        compiler_params=pltpu.CompilerParams(vmem_limit_bytes=20 * MIB),
        cost_estimate=pl.CostEstimate(
            flops=14_000_000_000, bytes_accessed=12_000_000, transcendentals=12_000_000
        ),
        name="own_part",
    )(limit, act, high, w_out)


def halo_part(limit, before, part, act, low, w_uvqk, w_out, out):
    half, width = low.shape
    head = width // HEADS
    scale = head ** (-0.5)
    reach = WINDOW // TILE

    def kernel(
        limit_ref, before_ref, part_ref, act, low_ref, w_in, wo_ref, _, out_ref, keyvals, done, w_ref, held, sums, sems
    ):
        stores = [
            pltpu.make_async_copy(
                done.at[pl.ds(i * TILE, TILE)], out_ref.at[pl.ds(i * TILE, TILE)], sems.at[i]
            )
            for i in range(reach)
        ]
        w_ref[...] = w_in[:, 2 * width :]
        mask = lower_mask()

        def project(m):
            rows = slice(m * TILE, (m + 1) * TILE)
            normed = normalize(before_ref[rows, :].astype(F32), 0.5).astype(BF16)
            for k in range(2):
                cols = slice(k * width, (k + 1) * width)
                keyvals[rows, cols] = silu_of_twice(dot(normed, w_ref[:, cols])).astype(BF16)

        def weigh(m, h, slot):
            scores = dot_nt(
                act[0 : (m + 1) * TILE, width + h * head : width + (h + 1) * head],
                keyvals[m * TILE : (m + 1) * TILE, h * head : (h + 1) * head],
            )
            weights = silu_of_twice(scores * (0.5 * scale))
            if m:
                held[slot, 0 : m * TILE, :] = weights[: m * TILE].astype(BF16)
            held[slot, m * TILE : (m + 1) * TILE, :] = jnp.where(mask, 0.0, weights[m * TILE :]).astype(BF16)

        def attend(m, h, slot):
            cols = slice(h * head, (h + 1) * head)
            rows = slice(0, (m + 1) * TILE)
            values = keyvals[m * TILE : (m + 1) * TILE, width + h * head : width + (h + 1) * head]
            so_far = part_ref if m + 1 == reach else sums
            sums[rows, cols] = so_far[rows, cols] + dot(held[slot, rows, :], values)

        units = [(m, h) for m in reversed(range(reach)) for h in range(HEADS)]
        project(reach - 1)
        for u in range(len(units) + 1):
            if u < len(units):
                weigh(*units[u], u % 2)
                if units[u][1] == 0 and units[u][0]:
                    project(units[u][0] - 1)
            if u == 0:
                continue
            m, h = units[u - 1]
            attend(m, h, (u - 1) % 2)
            if h + 1 < HEADS:
                continue
            rows = slice(m * TILE, (m + 1) * TILE)
            done[rows, :] = finish(
                sums[rows, :], act[rows, 0:width], low_ref[rows, :], wo_ref[...], limit_ref[0], m * TILE
            )
            stores[m].start()
        for store in stores:
            store.wait()

    return pl.pallas_call(
        kernel,
        out_shape=jax.ShapeDtypeStruct(out.shape, out.dtype),
        in_specs=[SMEM, VMEM, VMEM, VMEM, VMEM, VMEM, VMEM, ANY],
        out_specs=ANY,
        scratch_shapes=[
            pltpu.VMEM((half, 2 * width), BF16),
            pltpu.VMEM((half, width), BF16),
            pltpu.VMEM((width, 2 * width), BF16),
            pltpu.VMEM((2, WINDOW, TILE), BF16),
            pltpu.VMEM((half, width), F32),
            pltpu.SemaphoreType.DMA((reach,)),
        ],
        input_output_aliases={7: 0},
        compiler_params=pltpu.CompilerParams(vmem_limit_bytes=20 * MIB),
        name="halo_part",
    )(limit, before, part, act, low, w_uvqk, w_out, out)


def local(embed_table, lookup_ids, counts, event_order, hist_len, w_uvqk, w_out):
    shards = lax.axis_size("table")
    capacity = lookup_ids.shape[3]
    tokens = event_order.shape[2]
    width = embed_table.shape[1]
    parts = width // LANES
    exchange = lambda rows: lax.all_to_all(rows, "table", split_axis=0, concat_axis=0, tiled=True)
    stride = -(-capacity // LANES) * LANES
    starts_in_wide = jnp.pad(parts * lookup_ids[0, 0], ((0, 0), (0, stride - capacity)))
    requests = exchange(starts_in_wide.reshape(shards, stride // LANES, LANES)).reshape(shards * stride)
    fetched = exchange(gather_rows(embed_table, requests, shards, capacity, stride))
    live_counts = counts[0, 0]
    totals = jnp.cumsum(live_counts)
    starts = totals - live_counts
    event_rank = event_order[0, 0]
    owner_shard = jnp.sum((event_rank[:, None] >= totals[None, :]).astype(jnp.int32), axis=1)
    chosen = owner_shard[:, None] == jnp.arange(shards, dtype=jnp.int32)[None, :]
    slot_start = jnp.sum(jnp.where(chosen, starts[None, :], 0), axis=1)
    place = owner_shard * capacity + event_rank - slot_start
    low, high, act = project_rows(fetched.reshape(shards * capacity, width), parts * place, w_uvqk)
    before = passed_along(high, "seq", 1)
    limit = hist_len - lax.axis_index("seq") * tokens
    out, part = own_part(limit, act, high, w_out)
    result = halo_part(limit, before, part, act, low, w_uvqk, w_out, out)
    return result[None]


def solution(mesh):
    in_specs = (
        P("table", None),
        P("table", "seq", None, None),
        P("table", "seq", None),
        P("table", "seq", None),
        P("table"),
        P(),
        P(),
    )
    out_specs = P("table", "seq", None)
    return jax.shard_map(local, mesh=mesh, in_specs=in_specs, out_specs=out_specs, check_vma=False)
```
